128 devices in a mesh: sta: 16 (over y_hi, z, core), tpl: 8 (over y_lo, x).
Axes of the slice: x: 4, y: 4 (y_hi: 2, y_lo: 2; y = y_hi * 2 + y_lo), z: 4, core: 2. Of those that a mesh axis runs over, the one named last changes fastest.
Arguments:
- records: bfloat16 [16, 3, 32768], P('sta', None, 'tpl'), may hold values from -36 to 36
- templates: bfloat16 [256, 16, 3, 600], P('tpl', 'sta'), may hold values from -12 to 12
- moveouts: int32 [256, 16], P('tpl', 'sta'), may hold values from 0 to 63
Outputs:
- detection_stack: float32 [256, 16384], P('sta', 'tpl')
The draws below stay inside these ranges and needn't reach their ends.
Inputs may be any that keep to these rules, and one draw needn't show every extreme that they name: `moveouts`: lag offset at which station s joins the sum for template k.
All inputs are finite; a program needn't handle non-finite values.
Results may differ from the reference program's by a relative error of at most 0.0029.
Values may be sent and summed in bfloat16 or wider, within the bound.
A program may use at most 128 MiB of HBM per device.

```python
import math
import jax
import jax.numpy as jnp
from jax import lax

L = 600
COMP = 3
MAXSH = 64
K = 256
STATION_TOTAL = 16
RECORD_SAMPLES = 32768


def draw_records(key, part):
    noise_key = jax.random.fold_in(key, 11)
    gain_key = jax.random.fold_in(key, 12)
    spike_random_key = jax.random.fold_in(key, 13)
    noise = jax.random.truncated_normal(noise_key, -4.0, 4.0, (STATION_TOTAL, COMP, RECORD_SAMPLES), jnp.float32)
    gains = jnp.exp(jax.random.uniform(gain_key, (STATION_TOTAL, COMP, 1), jnp.float32, math.log(0.3), math.log(3.0)))
    spike_events = jnp.exp(jax.random.uniform(spike_random_key, (STATION_TOTAL, 1, RECORD_SAMPLES // 16), jnp.float32, math.log(0.3), math.log(3.0)))
    signal_envelope = jnp.repeat(spike_events, 16, axis=2)
    return (noise * gains * signal_envelope).astype(jnp.bfloat16)


def draw_templates(key, part):
    noise_key = jax.random.fold_in(key, 21)
    scale_key = jax.random.fold_in(key, 22)
    noise = jax.random.truncated_normal(noise_key, -4.0, 4.0, (K, STATION_TOTAL, COMP, L), jnp.float32)
    scales = jnp.exp(jax.random.uniform(scale_key, (K, STATION_TOTAL, COMP, 1), jnp.float32, math.log(0.3), math.log(3.0)))
    return (noise * scales).astype(jnp.bfloat16)


def plant(result, stream_key, low, largest):
    dims = result.shape
    spot = [jax.random.randint(jax.random.fold_in(stream_key, axis), (), 0, dims[axis]) for axis in range(len(dims))]
    result = result.at[tuple(spot)].set(low)
    longest = dims.index(max(dims))
    spot[longest] = (spot[longest] + 1) % dims[longest]
    return result.at[tuple(spot)].set(largest)


def setup_inputs(seed: int = 0) -> dict:
    arg_keys = jax.random.split(jax.random.key(seed), 4)
    records = draw_records(jax.random.fold_in(arg_keys[3], 71), 0)
    templates = draw_templates(jax.random.fold_in(arg_keys[3], 71), 0)
    moveouts = plant(jax.random.randint(arg_keys[2], (K, STATION_TOTAL), 0, MAXSH), jax.random.fold_in(arg_keys[2], 1), 0, MAXSH - 1).astype(jnp.int32)
    return dict(records=records, templates=templates, moveouts=moveouts)


def unit_templates(shape_block):
    as_float = shape_block.astype(jnp.float32)
    factor = lax.rsqrt(lax.optimization_barrier(jnp.mean(as_float * as_float, axis=3, keepdims=True)) + 1e-05)
    return (as_float * factor).astype(jnp.bfloat16)

def reference(records, templates, moveouts):
    stations = records.shape[0]
    length = templates.shape[3]
    rim_size = 2 * MAXSH + length - 2
    lag_total = records.shape[2] // 2
    span = lag_total + MAXSH
    extended = jnp.pad(records.astype(jnp.float32), ((0, 0), (0, 0), (0, rim_size)))
    sample_index = (2 * jnp.arange(span, dtype=jnp.int32)[None, :] + jnp.arange(length, dtype=jnp.int32)[:, None]).astype(jnp.int32)
    unit_shapes = unit_templates(templates).astype(jnp.float32)

    def arrival_pick_span(series, offset):
        return lax.dynamic_slice_in_dim(series, offset.astype(jnp.int32), lag_total, 0)

    def one_station(total, station):
        series = lax.dynamic_index_in_dim(extended, station, 0, keepdims=False)
        hankel = series[:, sample_index]
        energy = lax.optimization_barrier(jnp.sum(hankel * hankel, axis=1))
        scales = lax.rsqrt(energy / length + 1e-05) / length
        shapes = lax.dynamic_index_in_dim(unit_shapes, station, 1, keepdims=False)
        numerator = jnp.einsum('kcl,clw->kcw', shapes, hankel, precision=lax.Precision.HIGHEST)
        summed = lax.optimization_barrier(jnp.sum(numerator * scales[None, :, :], axis=1))
        offsets = lax.dynamic_index_in_dim(moveouts, station, 1, keepdims=False)
        windows = jax.vmap(arrival_pick_span)(summed, offsets)
        return (total + windows, station)
    initial = jnp.zeros((templates.shape[0], lag_total), jnp.float32)
    total, unused = lax.scan(one_station, initial, jnp.arange(stations, dtype=jnp.int32))
    return total
```

```python
import functools

import jax
import jax.numpy as jnp
from jax import lax
from jax.experimental import pallas as pl
from jax.experimental.pallas import tpu as pltpu
from jax.sharding import PartitionSpec as P

MESH = pl.DeviceIdType.MESH
F32, BF16 = jnp.float32, jnp.bfloat16
COMP = 3
LENGTH = 600
SEG = 4096
HALO = 768
WIDE = SEG + HALO
TAPS = 768
SPREAD = 256
SHARE = 32
HALF = 16
SUB = 8
ROWS = 256


def gather_kernel(rec_ref, tmpl_ref, mov_ref, all_ref, filt_ref, pick_ref, pad, send, recv, home):
    s, t = lax.axis_index("sta"), lax.axis_index("tpl")
    h = lax.rem(s, 2)
    barrier = pltpu.get_barrier_semaphore()
    for i in range(1, 8):
        pl.semaphore_signal(barrier, inc=1, device_id=(s, lax.rem(t + i, 8)), device_id_type=MESH)

    pad[...] = jnp.zeros_like(pad)
    moves = jnp.broadcast_to(mov_ref[...], (SHARE, TAPS))

    def filters(c):
        shape = tmpl_ref[:, c, :].astype(F32)
        factor = lax.rsqrt(jnp.sum(shape * shape, axis=1, keepdims=True) / LENGTH + 1e-05)
        pad[:, :LENGTH] = (shape * factor).astype(BF16).astype(F32)
        unit = pad[...]
        for bit in range(6):
            moved = pltpu.roll(unit, 2 << bit, 1)
            unit = jnp.where((moves & (1 << bit)) != 0, moved, unit)
        pad[...] = unit
        for part in range(2):
            first = pl.multiple_of(lax.rem(h + part, 2) * HALF, HALF)
            rows = pad[pl.ds(first, HALF), :]
            for b in range(SUB):
                moved = pltpu.roll(rows, 2 * b, 1) if b else rows
                at = part * HALF * SUB + b * HALF
                filt_ref[c, at : at + HALF, :] = moved.astype(BF16)
        pad[...] = jnp.zeros_like(pad)

    filters(0)
    pl.semaphore_wait(barrier, 7)
    copies = []
    for i in range(1, 8):
        copy = pltpu.make_async_remote_copy(
            src_ref=rec_ref,
            dst_ref=all_ref.at[t],
            send_sem=send.at[i],
            recv_sem=recv.at[t],
            device_id=(s, lax.rem(t + i, 8)),
            device_id_type=MESH,
        )
        copy.start()
        copies.append(copy)
    own = pltpu.make_async_copy(rec_ref, all_ref.at[t], home)
    own.start()
    filters(1)
    filters(2)
    lanes = lax.broadcasted_iota(jnp.int32, (HALF, SPREAD), 1) >> 1
    for part in range(2):
        first = pl.multiple_of(lax.rem(h + part, 2) * HALF, HALF)
        offsets = jnp.broadcast_to(mov_ref[pl.ds(first, HALF), :], (HALF, SPREAD))
        for b in range(SUB):
            at = part * HALF * SUB + b * HALF
            pick_ref[at : at + HALF, :] = jnp.where(lanes == offsets + b, 1.0, 0.0).astype(BF16)
    own.wait()
    for i in range(1, 8):
        copies[i - 1].wait_send()
        source = lax.rem(t + i, 8)
        pltpu.make_async_remote_copy(
            src_ref=rec_ref,
            dst_ref=all_ref.at[source],
            send_sem=send.at[i],
            recv_sem=recv.at[source],
            device_id=(s, source),
            device_id_type=MESH,
        ).wait_recv()


def gathered(rec, tmpl, mov):
    return pl.pallas_call(
        gather_kernel,
        out_shape=(
            jax.ShapeDtypeStruct((8, COMP, SEG), BF16),
            jax.ShapeDtypeStruct((COMP, ROWS, TAPS), BF16),
            jax.ShapeDtypeStruct((ROWS, SPREAD), BF16),
        ),
        in_specs=[pl.BlockSpec(memory_space=pltpu.VMEM)] * 3,
        out_specs=[pl.BlockSpec(memory_space=pltpu.VMEM)] * 3,
        scratch_shapes=[
            pltpu.VMEM((SHARE, TAPS), F32),
            pltpu.SemaphoreType.DMA((8,)),
            pltpu.SemaphoreType.DMA((8,)),
            pltpu.SemaphoreType.DMA,
        ],
        compiler_params=pltpu.CompilerParams(collective_id=1, has_side_effects=True, vmem_limit_bytes=32 << 20),
    )(rec, tmpl, mov)


def shifted_rows(row):
    wide = jnp.broadcast_to(row, (8, WIDE))
    low = pltpu.roll(wide, WIDE - 112, 1, stride=16, stride_axis=0)
    return jnp.concatenate([low[:, : WIDE - 128], low[:, 128:]], axis=0).astype(BF16)


def energy_scales(x):
    def ahead(v, n):
        return pltpu.roll(v, WIDE - n, 1)

    power = x * x
    two = power + ahead(power, 1)
    four = two + ahead(two, 2)
    eight = four + ahead(four, 4)
    sixteen = eight + ahead(eight, 8)
    far = sixteen + ahead(eight, 16)
    w32 = sixteen + ahead(sixteen, 16)
    w64 = w32 + ahead(w32, 32)
    w128 = w64 + ahead(w64, 64)
    w256 = w128 + ahead(w128, 128)
    w512 = w256 + ahead(w256, 256)
    energy = w512 + ahead(w64, 512) + ahead(far, 576)
    scale = lax.rsqrt(energy / LENGTH + 1e-05) / LENGTH
    high = scale.astype(BF16).astype(F32)
    low = (scale - high).astype(BF16).astype(F32)
    odd = (lax.broadcasted_iota(jnp.int32, x.shape, 1) & 1) == 1
    return jnp.where(odd, pltpu.roll(low, 1, 1), high)


def scan_kernel(all_ref, filt_ref, pick_ref, out_ref, x8, z8, base, own, part_out, part_in, sum_out, sum_in, cs, cr, ss, sr):
    s, t = lax.axis_index("sta"), lax.axis_index("tpl")
    h = lax.rem(s, 2)
    pair = lax.div(s, 2)
    sibling = (s + 1 - 2 * h, t)
    barrier = pltpu.get_barrier_semaphore()
    pl.semaphore_signal(barrier, inc=1, device_id=sibling, device_id_type=MESH)
    for j in range(8):

        @pl.when(jnp.logical_not((j == pair) & (pair == t)))
        def _():
            pl.semaphore_signal(barrier, inc=1, device_id=(2 * j + h, pair), device_id_type=MESH)

    for seg in range(8):
        block = all_ref[seg].astype(F32)
        for c in range(COMP):
            x8[c, seg : seg + 1, :SEG] = block[c : c + 1, :]
            if seg:
                x8[c, seg - 1 : seg, SEG:] = block[c : c + 1, :HALO]
    for c in range(COMP):
        x8[c, 7:8, SEG:] = jnp.zeros((1, HALO), F32)
    for c in range(COMP):
        z8[c] = energy_scales(x8[c])

    def core_copy(q):
        return pltpu.make_async_remote_copy(
            src_ref=part_out.at[q],
            dst_ref=part_in.at[q],
            send_sem=cs.at[q],
            recv_sem=cr.at[q],
            device_id=sibling,
            device_id_type=MESH,
        )

    def sum_copy(q):
        return pltpu.make_async_remote_copy(
            src_ref=sum_out.at[q],
            dst_ref=sum_in.at[pair],
            send_sem=ss.at[q],
            recv_sem=sr.at[pair],
            device_id=(2 * t + h, lax.rem(t + q, 8)),
            device_id_type=MESH,
        )

    def compute(q):
        seg = lax.rem(t + q, 8)
        for c in range(COMP):
            base[c, :, : WIDE - 128] = shifted_rows(x8[c, pl.ds(seg, 1), :])
            base[COMP + c, :, : WIDE - 128] = shifted_rows(z8[c, pl.ds(seg, 1), :])
        total = None
        for c in range(COMP):
            windows = jnp.concatenate([base[c, :, 256 * a : 256 * a + TAPS] for a in range(16)], axis=0)
            near = jnp.concatenate([base[COMP + c, :, 256 * a : 256 * a + SPREAD] for a in range(16)], axis=0)
            dims = (((1,), (1,)), ((), ()))
            number = lax.dot_general(windows, filt_ref[c], dims, preferred_element_type=F32)
            scale = lax.dot_general(near, pick_ref[...], dims, preferred_element_type=F32)
            term = number * scale
            total = term if total is None else total + term
        own[q] = total[:, :128]
        part_out[q] = total[:, 128:].astype(BF16)

    def finish(q):
        core_copy(q).wait_recv()
        both = (own[q] + part_in[q].astype(F32)).astype(BF16)
        seg = lax.rem(t + q, 8)
        mine = (pair == t) & (seg == t)

        @pl.when(mine)
        def _():
            sum_in[pair] = both

        @pl.when(jnp.logical_not(mine))
        def _():
            sum_out[q] = both
            sum_copy(q).start()

    compute(0)
    pl.semaphore_wait(barrier, 9 - (pair == t).astype(jnp.int32))
    core_copy(0).start()

    @pl.loop(1, 8)
    def _(q):
        compute(q)
        core_copy(q).start()
        finish(q - 1)

    finish(7)

    @pl.loop(0, 8)
    def _(q):
        core_copy(q).wait_send()

        @pl.when(jnp.logical_not((pair == t) & (lax.rem(t + q, 8) == t)))
        def _():
            sum_copy(q).wait_send()

    for j in range(8):

        @pl.when(jnp.logical_not((j == pair) & (pair == t)))
        def _():
            pltpu.make_async_remote_copy(
                src_ref=sum_out.at[j],
                dst_ref=sum_in.at[j],
                send_sem=ss.at[j],
                recv_sem=sr.at[j],
                device_id=(2 * t + h, t),
                device_id_type=MESH,
            ).wait_recv()

    total = sum_in[0].astype(F32)
    for j in range(1, 8):
        total = total + sum_in[j].astype(F32)
    out_ref[...] = total


def scanned(everything, filters, picks):
    return pl.pallas_call(
        scan_kernel,
        out_shape=jax.ShapeDtypeStruct((ROWS, 128), F32),
        in_specs=[pl.BlockSpec(memory_space=pltpu.VMEM)] * 3,
        out_specs=pl.BlockSpec(memory_space=pltpu.VMEM),
        scratch_shapes=[
            pltpu.VMEM((COMP, 8, WIDE), F32),
            pltpu.VMEM((COMP, 8, WIDE), F32),
            pltpu.VMEM((2 * COMP, 16, WIDE), BF16),
            pltpu.VMEM((8, ROWS, 128), F32),
            pltpu.VMEM((8, ROWS, 128), BF16),
            pltpu.VMEM((8, ROWS, 128), BF16),
            pltpu.VMEM((8, ROWS, 128), BF16),
            pltpu.VMEM((8, ROWS, 128), BF16),
            pltpu.SemaphoreType.DMA((8,)),
            pltpu.SemaphoreType.DMA((8,)),
            pltpu.SemaphoreType.DMA((8,)),
            pltpu.SemaphoreType.DMA((8,)),
        ],
        compiler_params=pltpu.CompilerParams(collective_id=2, has_side_effects=True, vmem_limit_bytes=48 << 20),
    )(everything, filters, picks)


def local(records, templates, moveouts):
    everything, filters, picks = gathered(records[0], templates[:, 0], moveouts)
    sums = scanned(everything, filters, picks)
    parts = jnp.flip(sums.reshape(ROWS // 8, 8, SUB, HALF), axis=1)
    return jnp.transpose(parts, (3, 0, 1, 2)).reshape(HALF, ROWS * SUB)


def solution(mesh):
    return jax.shard_map(
        local,
        mesh=mesh,
        in_specs=(P("sta", None, "tpl"), P("tpl", "sta", None, None), P("tpl", "sta")),
        out_specs=P("sta", "tpl"),
        check_vma=False,
    )
```

```python
import functools

import jax
import jax.numpy as jnp
from jax import lax
from jax.experimental import pallas as pl
from jax.experimental.pallas import tpu as pltpu
from jax.sharding import PartitionSpec as P

MESH = pl.DeviceIdType.MESH
F32, BF16 = jnp.float32, jnp.bfloat16
COMP = 3
LENGTH = 600
SEG = 4096
HALO = 768
WIDE = SEG + HALO
TAPS = 768
SPREAD = 256
SHARE = 32
HALF = 16
SUB = 8
ROWS = 256


def gather_kernel(rec_hbm, tmpl_hbm, mov_hbm, all_ref, filt_ref, pick_ref, tmpl_ref, mov_row, mov_ref, pad, send, recv, home):
    s, t = lax.axis_index("sta"), lax.axis_index("tpl")
    h = lax.rem(s, 2)
    barrier = pltpu.get_barrier_semaphore()
    for i in range(1, 8):
        pl.semaphore_signal(barrier, inc=1, device_id=(s, lax.rem(t + i, 8)), device_id_type=MESH)

    own = pltpu.make_async_copy(rec_hbm, all_ref.at[t], home.at[0])
    own.start()
    tmpl = pltpu.make_async_copy(tmpl_hbm, tmpl_ref, home.at[1])
    tmpl.start()
    shift = pltpu.make_async_copy(mov_hbm, mov_row, home.at[2])
    shift.start()
    pad[...] = jnp.zeros_like(pad)
    shift.wait()
    square = (SHARE, SHARE)
    diagonal = lax.broadcasted_iota(jnp.int32, square, 0) == lax.broadcasted_iota(jnp.int32, square, 1)
    mov_ref[...] = jnp.sum(jnp.where(diagonal, jnp.broadcast_to(mov_row[...], square), 0), axis=1, keepdims=True)
    moves = jnp.broadcast_to(mov_ref[...], (SHARE, TAPS))
    tmpl.wait()

    def filters(c):
        shape = tmpl_ref[c].astype(F32)
        factor = lax.rsqrt(jnp.sum(shape * shape, axis=1, keepdims=True) / LENGTH + 1e-05)
        pad[:, :LENGTH] = (shape * factor).astype(BF16).astype(F32)
        unit = pad[...]
        for bit in range(6):
            moved = pltpu.roll(unit, 2 << bit, 1)
            unit = jnp.where((moves & (1 << bit)) != 0, moved, unit)
        pad[...] = unit
        for part in range(2):
            first = pl.multiple_of(lax.rem(h + part, 2) * HALF, HALF)
            rows = pad[pl.ds(first, HALF), :]
            for b in range(SUB):
                moved = pltpu.roll(rows, 2 * b, 1) if b else rows
                at = part * HALF * SUB + b * HALF
                filt_ref[c, at : at + HALF, :] = moved.astype(BF16)
        pad[...] = jnp.zeros_like(pad)

    filters(0)
    own.wait()
    pl.semaphore_wait(barrier, 7)
    copies = []
    for i in range(1, 8):
        copy = pltpu.make_async_remote_copy(
            src_ref=all_ref.at[t],
            dst_ref=all_ref.at[t],
            send_sem=send.at[i],
            recv_sem=recv.at[t],
            device_id=(s, lax.rem(t + i, 8)),
            device_id_type=MESH,
        )
        copy.start()
        copies.append(copy)
    filters(1)
    filters(2)
    lanes = lax.broadcasted_iota(jnp.int32, (HALF, SPREAD), 1) >> 1
    for part in range(2):
        first = pl.multiple_of(lax.rem(h + part, 2) * HALF, HALF)
        offsets = jnp.broadcast_to(mov_ref[pl.ds(first, HALF), :], (HALF, SPREAD))
        for b in range(SUB):
            at = part * HALF * SUB + b * HALF
            pick_ref[at : at + HALF, :] = jnp.where(lanes == offsets + b, 1.0, 0.0).astype(BF16)
    for i in range(1, 8):
        copies[i - 1].wait_send()
        source = lax.rem(t + i, 8)
        pltpu.make_async_remote_copy(
            src_ref=all_ref.at[t],
            dst_ref=all_ref.at[source],
            send_sem=send.at[i],
            recv_sem=recv.at[source],
            device_id=(s, source),
            device_id_type=MESH,
        ).wait_recv()


def gathered(rec, tmpl, mov):
    return pl.pallas_call(
        gather_kernel,
        out_shape=(
            jax.ShapeDtypeStruct((8, COMP, SEG), BF16),
            jax.ShapeDtypeStruct((COMP, ROWS, TAPS), BF16),
            jax.ShapeDtypeStruct((ROWS, SPREAD), BF16),
        ),
        in_specs=[pl.BlockSpec(memory_space=pltpu.HBM)] * 3,
        out_specs=[pl.BlockSpec(memory_space=pltpu.VMEM)] * 3,
        scratch_shapes=[
            pltpu.VMEM((COMP, SHARE, LENGTH), BF16),
            pltpu.VMEM((1, SHARE), jnp.int32),
            pltpu.VMEM((SHARE, 1), jnp.int32),
            pltpu.VMEM((SHARE, TAPS), F32),
            pltpu.SemaphoreType.DMA((8,)),
            pltpu.SemaphoreType.DMA((8,)),
            pltpu.SemaphoreType.DMA((3,)),
        ],
        compiler_params=pltpu.CompilerParams(collective_id=1, has_side_effects=True, vmem_limit_bytes=32 << 20),
    )(rec, tmpl, mov)


def shifted_rows(row):
    wide = jnp.broadcast_to(row, (8, WIDE))
    low = pltpu.roll(wide, WIDE - 112, 1, stride=16, stride_axis=0)
    return jnp.concatenate([low[:, : WIDE - 128], low[:, 128:]], axis=0).astype(BF16)


def energy_scales(x):
    def ahead(v, n):
        return pltpu.roll(v, WIDE - n, 1)

    power = x * x
    two = power + ahead(power, 1)
    four = two + ahead(two, 2)
    eight = four + ahead(four, 4)
    sixteen = eight + ahead(eight, 8)
    far = sixteen + ahead(eight, 16)
    w32 = sixteen + ahead(sixteen, 16)
    w64 = w32 + ahead(w32, 32)
    w128 = w64 + ahead(w64, 64)
    w256 = w128 + ahead(w128, 128)
    w512 = w256 + ahead(w256, 256)
    energy = w512 + ahead(w64, 512) + ahead(far, 576)
    scale = lax.rsqrt(energy / LENGTH + 1e-05) / LENGTH
    high = scale.astype(BF16).astype(F32)
    low = (scale - high).astype(BF16).astype(F32)
    odd = (lax.broadcasted_iota(jnp.int32, x.shape, 1) & 1) == 1
    return jnp.where(odd, pltpu.roll(low, 1, 1), high)


def scan_kernel(all_ref, filt_ref, pick_ref, out_ref, x8, z8, base, own, part_out, part_in, sum_out, sum_in, cs, cr, ss, sr):
    s, t = lax.axis_index("sta"), lax.axis_index("tpl")
    h = lax.rem(s, 2)
    pair = lax.div(s, 2)
    sibling = (s + 1 - 2 * h, t)
    barrier = pltpu.get_barrier_semaphore()
    pl.semaphore_signal(barrier, inc=1, device_id=sibling, device_id_type=MESH)
    for j in range(8):

        @pl.when(jnp.logical_not((j == pair) & (pair == t)))
        def _():
            pl.semaphore_signal(barrier, inc=1, device_id=(2 * j + h, pair), device_id_type=MESH)

    for seg in range(8):
        block = all_ref[seg].astype(F32)
        for c in range(COMP):
            x8[c, seg : seg + 1, :SEG] = block[c : c + 1, :]
            if seg:
                x8[c, seg - 1 : seg, SEG:] = block[c : c + 1, :HALO]
    for c in range(COMP):
        x8[c, 7:8, SEG:] = jnp.zeros((1, HALO), F32)
    for c in range(COMP):
        z8[c] = energy_scales(x8[c])

    def core_copy(q):
        return pltpu.make_async_remote_copy(
            src_ref=part_out.at[q],
            dst_ref=part_in.at[q],
            send_sem=cs.at[q],
            recv_sem=cr.at[q],
            device_id=sibling,
            device_id_type=MESH,
        )

    def sum_copy(q):
        return pltpu.make_async_remote_copy(
            src_ref=sum_out.at[q],
            dst_ref=sum_in.at[pair],
            send_sem=ss.at[q],
            recv_sem=sr.at[pair],
            device_id=(2 * t + h, lax.rem(pair + q, 8)),
            device_id_type=MESH,
        )

    def compute(q):
        seg = lax.rem(pair + q, 8)
        for c in range(COMP):
            base[c, :, : WIDE - 128] = shifted_rows(x8[c, pl.ds(seg, 1), :])
            base[COMP + c, :, : WIDE - 128] = shifted_rows(z8[c, pl.ds(seg, 1), :])
        total = None
        for c in range(COMP):
            windows = jnp.concatenate([base[c, :, 256 * a : 256 * a + TAPS] for a in range(16)], axis=0)
            near = jnp.concatenate([base[COMP + c, :, 256 * a : 256 * a + SPREAD] for a in range(16)], axis=0)
            dims = (((1,), (1,)), ((), ()))
            number = lax.dot_general(windows, filt_ref[c], dims, preferred_element_type=F32)
            scale = lax.dot_general(near, pick_ref[...], dims, preferred_element_type=F32)
            term = number * scale
            total = term if total is None else total + term
        own[q] = total[:, :128]
        part_out[q] = total[:, 128:].astype(BF16)

    def finish(q):
        core_copy(q).wait_recv()
        both = (own[q] + part_in[q].astype(F32)).astype(BF16)
        seg = lax.rem(pair + q, 8)
        mine = (pair == t) & (seg == t)

        @pl.when(mine)
        def _():
            sum_in[pair] = both

        @pl.when(jnp.logical_not(mine))
        def _():
            sum_out[q] = both
            sum_copy(q).start()

    compute(0)
    pl.semaphore_wait(barrier, 9 - (pair == t).astype(jnp.int32))
    core_copy(0).start()

    @pl.loop(1, 8)
    def _(q):
        compute(q)
        core_copy(q).start()
        finish(q - 1)

    finish(7)

    @pl.loop(0, 8)
    def _(q):
        core_copy(q).wait_send()

        @pl.when(jnp.logical_not((pair == t) & (lax.rem(pair + q, 8) == t)))
        def _():
            sum_copy(q).wait_send()

    for j in range(8):

        @pl.when(jnp.logical_not((j == pair) & (pair == t)))
        def _():
            pltpu.make_async_remote_copy(
                src_ref=sum_out.at[j],
                dst_ref=sum_in.at[j],
                send_sem=ss.at[j],
                recv_sem=sr.at[j],
                device_id=(2 * t + h, t),
                device_id_type=MESH,
            ).wait_recv()

    total = sum_in[0].astype(F32)
    for j in range(1, 8):
        total = total + sum_in[j].astype(F32)
    out_ref[...] = total


def scanned(everything, filters, picks):
    return pl.pallas_call(
        scan_kernel,
        out_shape=jax.ShapeDtypeStruct((ROWS, 128), F32),
        in_specs=[pl.BlockSpec(memory_space=pltpu.VMEM)] * 3,
        out_specs=pl.BlockSpec(memory_space=pltpu.VMEM),
        scratch_shapes=[
            pltpu.VMEM((COMP, 8, WIDE), F32),
            pltpu.VMEM((COMP, 8, WIDE), F32),
            pltpu.VMEM((2 * COMP, 16, WIDE), BF16),
            pltpu.VMEM((8, ROWS, 128), F32),
            pltpu.VMEM((8, ROWS, 128), BF16),
            pltpu.VMEM((8, ROWS, 128), BF16),
            pltpu.VMEM((8, ROWS, 128), BF16),
            pltpu.VMEM((8, ROWS, 128), BF16),
            pltpu.SemaphoreType.DMA((8,)),
            pltpu.SemaphoreType.DMA((8,)),
            pltpu.SemaphoreType.DMA((8,)),
            pltpu.SemaphoreType.DMA((8,)),
        ],
        compiler_params=pltpu.CompilerParams(collective_id=2, has_side_effects=True, vmem_limit_bytes=48 << 20),
    )(everything, filters, picks)


def local(records, templates, moveouts):
    operands = (records[0], jnp.transpose(templates[:, 0], (1, 0, 2)), jnp.transpose(moveouts))
    everything, filters, picks = gathered(*[pltpu.with_memory_space_constraint(v, pltpu.HBM) for v in operands])
    sums = scanned(everything, filters, picks)
    parts = jnp.flip(sums.reshape(ROWS // 8, 8, SUB, HALF), axis=1)
    return jnp.transpose(parts, (3, 0, 1, 2)).reshape(HALF, ROWS * SUB)


def solution(mesh):
    return jax.shard_map(
        local,
        mesh=mesh,
        in_specs=(P("sta", None, "tpl"), P("tpl", "sta", None, None), P("tpl", "sta")),
        out_specs=P("sta", "tpl"),
        check_vma=False,
    )
```

```python
import functools

import jax
import jax.numpy as jnp
from jax import lax
from jax.experimental import pallas as pl
from jax.experimental.pallas import tpu as pltpu
from jax.sharding import PartitionSpec as P

MESH = pl.DeviceIdType.MESH
F32, BF16 = jnp.float32, jnp.bfloat16
COMP = 3
LENGTH = 600
SEG = 4096
HALO = 768
WIDE = SEG + HALO
TAPS = 768
SPREAD = 256
SHARE = 32
HALF = 16
SUB = 8
ROWS = 256
ORDER = (6, 7, 5, 2, 4, 3, 1)
NEAR = (6, 7, 5, 2, 4, 3, 1, 0)


def gather_kernel(rec_hbm, tmpl_hbm, mov_hbm, all_ref, filt_ref, pick_ref, tmpl_ref, mov_row, mov_ref, pad, send, recv, home):
    s, t = lax.axis_index("sta"), lax.axis_index("tpl")
    h = lax.rem(s, 2)
    barrier = pltpu.get_barrier_semaphore()
    for i in ORDER:
        pl.semaphore_signal(barrier, inc=1, device_id=(s, t ^ i), device_id_type=MESH)

    own = pltpu.make_async_copy(rec_hbm, all_ref.at[t], home.at[0])
    own.start()
    tmpl = pltpu.make_async_copy(tmpl_hbm, tmpl_ref, home.at[1])
    tmpl.start()
    shift = pltpu.make_async_copy(mov_hbm, mov_row, home.at[2])
    shift.start()
    pad[...] = jnp.zeros_like(pad)
    shift.wait()
    square = (SHARE, SHARE)
    diagonal = lax.broadcasted_iota(jnp.int32, square, 0) == lax.broadcasted_iota(jnp.int32, square, 1)
    mov_ref[...] = jnp.sum(jnp.where(diagonal, jnp.broadcast_to(mov_row[...], square), 0), axis=1, keepdims=True)
    moves = jnp.broadcast_to(mov_ref[...], (SHARE, TAPS))
    tmpl.wait()

    def filters(c):
        shape = tmpl_ref[c].astype(F32)
        factor = lax.rsqrt(jnp.sum(shape * shape, axis=1, keepdims=True) / LENGTH + 1e-05)
        pad[:, :LENGTH] = (shape * factor).astype(BF16).astype(F32)
        unit = pad[...]
        for bit in range(6):
            moved = pltpu.roll(unit, 2 << bit, 1)
            unit = jnp.where((moves & (1 << bit)) != 0, moved, unit)
        pad[...] = unit
        for part in range(2):
            first = pl.multiple_of(lax.rem(h + part, 2) * HALF, HALF)
            rows = pad[pl.ds(first, HALF), :]
            for b in range(SUB):
                moved = pltpu.roll(rows, 2 * b, 1) if b else rows
                at = part * HALF * SUB + b * HALF
                filt_ref[c, at : at + HALF, :] = moved.astype(BF16)
        pad[...] = jnp.zeros_like(pad)

    filters(0)
    own.wait()
    pl.semaphore_wait(barrier, 7)
    copies = []
    for i in ORDER:
        copy = pltpu.make_async_remote_copy(
            src_ref=all_ref.at[t],
            dst_ref=all_ref.at[t],
            send_sem=send.at[i],
            recv_sem=recv.at[t],
            device_id=(s, t ^ i),
            device_id_type=MESH,
        )
        copy.start()
        copies.append(copy)
    filters(1)
    filters(2)
    lanes = lax.broadcasted_iota(jnp.int32, (HALF, SPREAD), 1) >> 1
    for part in range(2):
        first = pl.multiple_of(lax.rem(h + part, 2) * HALF, HALF)
        offsets = jnp.broadcast_to(mov_ref[pl.ds(first, HALF), :], (HALF, SPREAD))
        for b in range(SUB):
            at = part * HALF * SUB + b * HALF
            pick_ref[at : at + HALF, :] = jnp.where(lanes == offsets + b, 1.0, 0.0).astype(BF16)
    for copy in copies:
        copy.wait_send()
    for i in ORDER:
        source = t ^ i
        pltpu.make_async_remote_copy(
            src_ref=all_ref.at[t],
            dst_ref=all_ref.at[source],
            send_sem=send.at[i],
            recv_sem=recv.at[source],
            device_id=(s, source),
            device_id_type=MESH,
        ).wait_recv()


def gathered(rec, tmpl, mov):
    return pl.pallas_call(
        gather_kernel,
        out_shape=(
            jax.ShapeDtypeStruct((8, COMP, SEG), BF16),
            jax.ShapeDtypeStruct((COMP, ROWS, TAPS), BF16),
            jax.ShapeDtypeStruct((ROWS, SPREAD), BF16),
        ),
        in_specs=[pl.BlockSpec(memory_space=pltpu.HBM)] * 3,
        out_specs=[pl.BlockSpec(memory_space=pltpu.VMEM)] * 3,
        scratch_shapes=[
            pltpu.VMEM((COMP, SHARE, LENGTH), BF16),
            pltpu.VMEM((1, SHARE), jnp.int32),
            pltpu.VMEM((SHARE, 1), jnp.int32),
            pltpu.VMEM((SHARE, TAPS), F32),
            pltpu.SemaphoreType.DMA((8,)),
            pltpu.SemaphoreType.DMA((8,)),
            pltpu.SemaphoreType.DMA((3,)),
        ],
        compiler_params=pltpu.CompilerParams(collective_id=1, has_side_effects=True, vmem_limit_bytes=32 << 20),
    )(rec, tmpl, mov)


def shifted_rows(row):
    wide = jnp.broadcast_to(row, (8, WIDE))
    low = pltpu.roll(wide, WIDE - 112, 1, stride=16, stride_axis=0)
    return jnp.concatenate([low[:, : WIDE - 128], low[:, 128:]], axis=0).astype(BF16)


def energy_scales(x):
    def ahead(v, n):
        return pltpu.roll(v, WIDE - n, 1)

    power = x * x
    two = power + ahead(power, 1)
    four = two + ahead(two, 2)
    eight = four + ahead(four, 4)
    sixteen = eight + ahead(eight, 8)
    far = sixteen + ahead(eight, 16)
    w32 = sixteen + ahead(sixteen, 16)
    w64 = w32 + ahead(w32, 32)
    w128 = w64 + ahead(w64, 64)
    w256 = w128 + ahead(w128, 128)
    w512 = w256 + ahead(w256, 256)
    energy = w512 + ahead(w64, 512) + ahead(far, 576)
    scale = lax.rsqrt(energy / LENGTH + 1e-05) / LENGTH
    high = scale.astype(BF16).astype(F32)
    low = (scale - high).astype(BF16).astype(F32)
    odd = (lax.broadcasted_iota(jnp.int32, x.shape, 1) & 1) == 1
    return jnp.where(odd, pltpu.roll(low, 1, 1), high)


def scan_kernel(all_ref, filt_ref, pick_ref, out_ref, x8, z8, base, own, part_out, part_in, sum_out, sum_in, cs, cr, ss, sr):
    s, t = lax.axis_index("sta"), lax.axis_index("tpl")
    h = lax.rem(s, 2)
    pair = lax.div(s, 2)
    sibling = (s + 1 - 2 * h, t)
    barrier = pltpu.get_barrier_semaphore()
    pl.semaphore_signal(barrier, inc=1, device_id=sibling, device_id_type=MESH)
    for i in NEAR:
        j = pair ^ i

        @pl.when(jnp.logical_not((j == pair) & (pair == t)))
        def _():
            pl.semaphore_signal(barrier, inc=1, device_id=(2 * j + h, pair), device_id_type=MESH)

    for seg in range(8):
        block = all_ref[seg].astype(F32)
        for c in range(COMP):
            x8[c, seg : seg + 1, :SEG] = block[c : c + 1, :]
            if seg:
                x8[c, seg - 1 : seg, SEG:] = block[c : c + 1, :HALO]
    for c in range(COMP):
        x8[c, 7:8, SEG:] = jnp.zeros((1, HALO), F32)
    for c in range(COMP):
        z8[c] = energy_scales(x8[c])

    def core_copy(q):
        return pltpu.make_async_remote_copy(
            src_ref=part_out.at[q],
            dst_ref=part_in.at[q],
            send_sem=cs.at[q],
            recv_sem=cr.at[q],
            device_id=sibling,
            device_id_type=MESH,
        )

    def sum_copy(q):
        return pltpu.make_async_remote_copy(
            src_ref=sum_out.at[q],
            dst_ref=sum_in.at[pair],
            send_sem=ss.at[q],
            recv_sem=sr.at[pair],
            device_id=(2 * t + h, lax.rem(pair + q, 8)),
            device_id_type=MESH,
        )

    def compute(q):
        seg = lax.rem(pair + q, 8)
        for c in range(COMP):
            base[c, :, : WIDE - 128] = shifted_rows(x8[c, pl.ds(seg, 1), :])
            base[COMP + c, :, : WIDE - 128] = shifted_rows(z8[c, pl.ds(seg, 1), :])
        total = None
        for c in range(COMP):
            windows = jnp.concatenate([base[c, :, 256 * a : 256 * a + TAPS] for a in range(16)], axis=0)
            near = jnp.concatenate([base[COMP + c, :, 256 * a : 256 * a + SPREAD] for a in range(16)], axis=0)
            dims = (((1,), (1,)), ((), ()))
            number = lax.dot_general(windows, filt_ref[c], dims, preferred_element_type=F32)
            scale = lax.dot_general(near, pick_ref[...], dims, preferred_element_type=F32)
            term = number * scale
            total = term if total is None else total + term
        own[q] = total[:, :128]
        part_out[q] = total[:, 128:].astype(BF16)

    def finish(q):
        core_copy(q).wait_recv()
        both = (own[q] + part_in[q].astype(F32)).astype(BF16)
        seg = lax.rem(pair + q, 8)
        mine = (pair == t) & (seg == t)

        @pl.when(mine)
        def _():
            sum_in[pair] = both

        @pl.when(jnp.logical_not(mine))
        def _():
            sum_out[q] = both
            sum_copy(q).start()

    compute(0)
    pl.semaphore_wait(barrier, 9 - (pair == t).astype(jnp.int32))
    core_copy(0).start()

    @pl.loop(1, 8)
    def _(q):
        compute(q)
        core_copy(q).start()
        finish(q - 1)

    finish(7)

    @pl.loop(0, 8)
    def _(q):
        core_copy(q).wait_send()

        @pl.when(jnp.logical_not((pair == t) & (lax.rem(pair + q, 8) == t)))
        def _():
            sum_copy(q).wait_send()

    for j in range(8):

        @pl.when(jnp.logical_not((j == pair) & (pair == t)))
        def _():
            pltpu.make_async_remote_copy(
                src_ref=sum_out.at[j],
                dst_ref=sum_in.at[j],
                send_sem=ss.at[j],
                recv_sem=sr.at[j],
                device_id=(2 * t + h, t),
                device_id_type=MESH,
            ).wait_recv()

    total = sum_in[0].astype(F32)
    for j in range(1, 8):
        total = total + sum_in[j].astype(F32)
    out_ref[...] = total


def scanned(everything, filters, picks):
    return pl.pallas_call(
        scan_kernel,
        out_shape=jax.ShapeDtypeStruct((ROWS, 128), F32),
        in_specs=[pl.BlockSpec(memory_space=pltpu.VMEM)] * 3,
        out_specs=pl.BlockSpec(memory_space=pltpu.VMEM),
        scratch_shapes=[
            pltpu.VMEM((COMP, 8, WIDE), F32),
            pltpu.VMEM((COMP, 8, WIDE), F32),
            pltpu.VMEM((2 * COMP, 16, WIDE), BF16),
            pltpu.VMEM((8, ROWS, 128), F32),
            pltpu.VMEM((8, ROWS, 128), BF16),
            pltpu.VMEM((8, ROWS, 128), BF16),
            pltpu.VMEM((8, ROWS, 128), BF16),
            pltpu.VMEM((8, ROWS, 128), BF16),
            pltpu.SemaphoreType.DMA((8,)),
            pltpu.SemaphoreType.DMA((8,)),
            pltpu.SemaphoreType.DMA((8,)),
            pltpu.SemaphoreType.DMA((8,)),
        ],
        compiler_params=pltpu.CompilerParams(collective_id=2, has_side_effects=True, vmem_limit_bytes=48 << 20),
    )(everything, filters, picks)


def local(records, templates, moveouts):
    operands = (records[0], jnp.transpose(templates[:, 0], (1, 0, 2)), jnp.transpose(moveouts))
    everything, filters, picks = gathered(*[pltpu.with_memory_space_constraint(v, pltpu.HBM) for v in operands])
    sums = scanned(everything, filters, picks)
    parts = jnp.flip(sums.reshape(ROWS // 8, 8, SUB, HALF), axis=1)
    return jnp.transpose(parts, (3, 0, 1, 2)).reshape(HALF, ROWS * SUB)


def solution(mesh):
    return jax.shard_map(
        local,
        mesh=mesh,
        in_specs=(P("sta", None, "tpl"), P("tpl", "sta", None, None), P("tpl", "sta")),
        out_specs=P("sta", "tpl"),
        check_vma=False,
    )
```

```python
import functools

import jax
import jax.numpy as jnp
from jax import lax
from jax.experimental import pallas as pl
from jax.experimental.pallas import tpu as pltpu
from jax.sharding import PartitionSpec as P

MESH = pl.DeviceIdType.MESH
F32, BF16 = jnp.float32, jnp.bfloat16
COMP = 3
LENGTH = 600
SEG = 4096
HALO = 768
WIDE = SEG + HALO
TAPS = 768
SPREAD = 256
SHARE = 32
HALF = 16
SUB = 8
ROWS = 256
ORDER = (6, 7, 5, 2, 4, 3, 1)
NEAR = (6, 7, 5, 2, 4, 3, 1, 0)


def gather_kernel(rec_hbm, tmpl_hbm, mov_hbm, all_ref, filt_ref, pick_ref, tmpl_ref, mov_row, mov_ref, pad, send, recv, home):
    s, t = lax.axis_index("sta"), lax.axis_index("tpl")
    h = lax.rem(s, 2)
    barrier = pltpu.get_barrier_semaphore()
    for i in ORDER:
        pl.semaphore_signal(barrier, inc=1, device_id=(s, t ^ i), device_id_type=MESH)

    own = pltpu.make_async_copy(rec_hbm, all_ref.at[t], home.at[0])
    own.start()
    tmpl = pltpu.make_async_copy(tmpl_hbm, tmpl_ref, home.at[1])
    tmpl.start()
    shift = pltpu.make_async_copy(mov_hbm, mov_row, home.at[2])
    shift.start()
    pad[...] = jnp.zeros_like(pad)
    shift.wait()
    square = (SHARE, SHARE)
    diagonal = lax.broadcasted_iota(jnp.int32, square, 0) == lax.broadcasted_iota(jnp.int32, square, 1)
    mov_ref[...] = jnp.sum(jnp.where(diagonal, jnp.broadcast_to(mov_row[...], square), 0), axis=1, keepdims=True)
    moves = jnp.broadcast_to(mov_ref[...], (SHARE, TAPS))
    tmpl.wait()

    def filters(c):
        shape = tmpl_ref[c].astype(F32)
        factor = lax.rsqrt(jnp.sum(shape * shape, axis=1, keepdims=True) / LENGTH + 1e-05)
        pad[:, :LENGTH] = (shape * factor).astype(BF16).astype(F32)
        unit = pad[...]
        for bit in range(6):
            moved = pltpu.roll(unit, 2 << bit, 1)
            unit = jnp.where((moves & (1 << bit)) != 0, moved, unit)
        pad[...] = unit
        for part in range(2):
            first = pl.multiple_of(lax.rem(h + part, 2) * HALF, HALF)
            rows = pad[pl.ds(first, HALF), :]
            for b in range(SUB):
                moved = pltpu.roll(rows, 2 * b, 1) if b else rows
                at = part * HALF * SUB + b * HALF
                filt_ref[c, at : at + HALF, :] = moved.astype(BF16)
        pad[...] = jnp.zeros_like(pad)

    filters(0)
    own.wait()
    pl.semaphore_wait(barrier, 7)
    copies = []
    for i in ORDER:
        copy = pltpu.make_async_remote_copy(
            src_ref=all_ref.at[t],
            dst_ref=all_ref.at[t],
            send_sem=send.at[i],
            recv_sem=recv.at[t],
            device_id=(s, t ^ i),
            device_id_type=MESH,
        )
        copy.start()
        copies.append(copy)
    filters(1)
    filters(2)
    lanes = lax.broadcasted_iota(jnp.int32, (HALF, SPREAD), 1) >> 1
    for part in range(2):
        first = pl.multiple_of(lax.rem(h + part, 2) * HALF, HALF)
        offsets = jnp.broadcast_to(mov_ref[pl.ds(first, HALF), :], (HALF, SPREAD))
        for b in range(SUB):
            at = part * HALF * SUB + b * HALF
            pick_ref[at : at + HALF, :] = jnp.where(lanes == offsets + b, 1.0, 0.0).astype(BF16)
    for copy in copies:
        copy.wait_send()
    for i in ORDER:
        source = t ^ i
        pltpu.make_async_remote_copy(
            src_ref=all_ref.at[t],
            dst_ref=all_ref.at[source],
            send_sem=send.at[i],
            recv_sem=recv.at[source],
            device_id=(s, source),
            device_id_type=MESH,
        ).wait_recv()


def gathered(rec, tmpl, mov):
    return pl.pallas_call(
        gather_kernel,
        out_shape=(
            jax.ShapeDtypeStruct((8, COMP, SEG), BF16),
            jax.ShapeDtypeStruct((COMP, ROWS, TAPS), BF16),
            jax.ShapeDtypeStruct((ROWS, SPREAD), BF16),
        ),
        in_specs=[pl.BlockSpec(memory_space=pltpu.HBM)] * 3,
        out_specs=[pl.BlockSpec(memory_space=pltpu.VMEM)] * 3,
        scratch_shapes=[
            pltpu.VMEM((COMP, SHARE, LENGTH), BF16),
            pltpu.VMEM((1, SHARE), jnp.int32),
            pltpu.VMEM((SHARE, 1), jnp.int32),
            pltpu.VMEM((SHARE, TAPS), F32),
            pltpu.SemaphoreType.DMA((8,)),
            pltpu.SemaphoreType.DMA((8,)),
            pltpu.SemaphoreType.DMA((3,)),
        ],
        compiler_params=pltpu.CompilerParams(collective_id=1, has_side_effects=True, vmem_limit_bytes=32 << 20),
    )(rec, tmpl, mov)


def shifted_rows(row):
    wide = jnp.broadcast_to(row, (8, WIDE))
    low = pltpu.roll(wide, WIDE - 112, 1, stride=16, stride_axis=0)
    return jnp.concatenate([low[:, : WIDE - 128], low[:, 128:]], axis=0).astype(BF16)


def energy_scales(x):
    def ahead(v, n):
        return pltpu.roll(v, WIDE - n, 1)

    power = x * x
    two = power + ahead(power, 1)
    four = two + ahead(two, 2)
    eight = four + ahead(four, 4)
    sixteen = eight + ahead(eight, 8)
    far = sixteen + ahead(eight, 16)
    w32 = sixteen + ahead(sixteen, 16)
    w64 = w32 + ahead(w32, 32)
    w128 = w64 + ahead(w64, 64)
    w256 = w128 + ahead(w128, 128)
    w512 = w256 + ahead(w256, 256)
    energy = w512 + ahead(w64, 512) + ahead(far, 576)
    scale = lax.rsqrt(energy / LENGTH + 1e-05) / LENGTH
    high = scale.astype(BF16).astype(F32)
    low = (scale - high).astype(BF16).astype(F32)
    odd = (lax.broadcasted_iota(jnp.int32, x.shape, 1) & 1) == 1
    return jnp.where(odd, pltpu.roll(low, 1, 1), high)


def scan_kernel(all_ref, filt_ref, pick_ref, out_ref, x8, z8, base, own, part_out, part_in, sum_out, sum_in, cs, cr, ss, sr):
    s, t = lax.axis_index("sta"), lax.axis_index("tpl")
    h = lax.rem(s, 2)
    pair = lax.div(s, 2)
    sibling = (s + 1 - 2 * h, t)
    barrier = pltpu.get_barrier_semaphore()
    pl.semaphore_signal(barrier, inc=1, device_id=sibling, device_id_type=MESH)
    for i in NEAR:
        j = pair ^ i

        @pl.when(jnp.logical_not((j == pair) & (pair == t)))
        def _():
            pl.semaphore_signal(barrier, inc=1, device_id=(2 * j + h, pair), device_id_type=MESH)

    for seg in range(8):
        block = all_ref[seg].astype(F32)
        for c in range(COMP):
            x8[c, seg : seg + 1, :SEG] = block[c : c + 1, :]
            if seg:
                x8[c, seg - 1 : seg, SEG:] = block[c : c + 1, :HALO]
    for c in range(COMP):
        x8[c, 7:8, SEG:] = jnp.zeros((1, HALO), F32)
    for c in range(COMP):
        z8[c] = energy_scales(x8[c])

    def core_copy(q):
        return pltpu.make_async_remote_copy(
            src_ref=part_out.at[q],
            dst_ref=part_in.at[q],
            send_sem=cs.at[q],
            recv_sem=cr.at[q],
            device_id=sibling,
            device_id_type=MESH,
        )

    def sum_copy(q):
        return pltpu.make_async_remote_copy(
            src_ref=sum_out.at[q],
            dst_ref=sum_in.at[pair],
            send_sem=ss.at[q],
            recv_sem=sr.at[pair],
            device_id=(2 * t + h, lax.rem(pair + q, 8)),
            device_id_type=MESH,
        )

    def compute(q):
        seg = lax.rem(pair + q, 8)
        for c in range(COMP):
            base[c, :, : WIDE - 128] = shifted_rows(x8[c, pl.ds(seg, 1), :])
            base[COMP + c, :, : WIDE - 128] = shifted_rows(z8[c, pl.ds(seg, 1), :])
        total = None
        for c in range(COMP):
            windows = jnp.concatenate([base[c, :, 256 * a : 256 * a + TAPS] for a in range(16)], axis=0)
            near = jnp.concatenate([base[COMP + c, :, 256 * a : 256 * a + SPREAD] for a in range(16)], axis=0)
            dims = (((1,), (1,)), ((), ()))
            number = lax.dot_general(windows, filt_ref[c], dims, preferred_element_type=F32)
            scale = lax.dot_general(near, pick_ref[...], dims, preferred_element_type=F32)
            term = number * scale
            total = term if total is None else total + term
        own[q] = total[:, :128]
        part_out[q] = total[:, 128:].astype(BF16)

    def finish(q):
        core_copy(q).wait_recv()
        both = (own[q] + part_in[q].astype(F32)).astype(BF16)
        seg = lax.rem(pair + q, 8)
        mine = (pair == t) & (seg == t)

        @pl.when(mine)
        def _():
            sum_in[pair] = both

        @pl.when(jnp.logical_not(mine))
        def _():
            sum_out[q] = both
            sum_copy(q).start()

    compute(0)
    pl.semaphore_wait(barrier, 9 - (pair == t).astype(jnp.int32))
    core_copy(0).start()

    compute(1)
    core_copy(1).start()

    @pl.loop(2, 8)
    def _(q):
        compute(q)
        core_copy(q).start()
        finish(q - 2)

    finish(6)
    finish(7)

    @pl.loop(0, 8)
    def _(q):
        core_copy(q).wait_send()

        @pl.when(jnp.logical_not((pair == t) & (lax.rem(pair + q, 8) == t)))
        def _():
            sum_copy(q).wait_send()

    for j in range(8):

        @pl.when(jnp.logical_not((j == pair) & (pair == t)))
        def _():
            pltpu.make_async_remote_copy(
                src_ref=sum_out.at[j],
                dst_ref=sum_in.at[j],
                send_sem=ss.at[j],
                recv_sem=sr.at[j],
                device_id=(2 * t + h, t),
                device_id_type=MESH,
            ).wait_recv()

    total = sum_in[0].astype(F32)
    for j in range(1, 8):
        total = total + sum_in[j].astype(F32)
    out_ref[...] = total


def scanned(everything, filters, picks):
    return pl.pallas_call(
        scan_kernel,
        out_shape=jax.ShapeDtypeStruct((ROWS, 128), F32),
        in_specs=[pl.BlockSpec(memory_space=pltpu.VMEM)] * 3,
        out_specs=pl.BlockSpec(memory_space=pltpu.VMEM),
        scratch_shapes=[
            pltpu.VMEM((COMP, 8, WIDE), F32),
            pltpu.VMEM((COMP, 8, WIDE), F32),
            pltpu.VMEM((2 * COMP, 16, WIDE), BF16),
            pltpu.VMEM((8, ROWS, 128), F32),
            pltpu.VMEM((8, ROWS, 128), BF16),
            pltpu.VMEM((8, ROWS, 128), BF16),
            pltpu.VMEM((8, ROWS, 128), BF16),
            pltpu.VMEM((8, ROWS, 128), BF16),
            pltpu.SemaphoreType.DMA((8,)),
            pltpu.SemaphoreType.DMA((8,)),
            pltpu.SemaphoreType.DMA((8,)),
            pltpu.SemaphoreType.DMA((8,)),
        ],
        compiler_params=pltpu.CompilerParams(collective_id=2, has_side_effects=True, vmem_limit_bytes=48 << 20),
    )(everything, filters, picks)


def local(records, templates, moveouts):
    operands = (records[0], jnp.transpose(templates[:, 0], (1, 0, 2)), jnp.transpose(moveouts))
    everything, filters, picks = gathered(*[pltpu.with_memory_space_constraint(v, pltpu.HBM) for v in operands])
    sums = scanned(everything, filters, picks)
    parts = jnp.flip(sums.reshape(ROWS // 8, 8, SUB, HALF), axis=1)
    return jnp.transpose(parts, (3, 0, 1, 2)).reshape(HALF, ROWS * SUB)


def solution(mesh):
    return jax.shard_map(
        local,
        mesh=mesh,
        in_specs=(P("sta", None, "tpl"), P("tpl", "sta", None, None), P("tpl", "sta")),
        out_specs=P("sta", "tpl"),
        check_vma=False,
    )
```

```python
import functools

import jax
import jax.numpy as jnp
from jax import lax
from jax.experimental import pallas as pl
from jax.experimental.pallas import tpu as pltpu
from jax.sharding import PartitionSpec as P

MESH = pl.DeviceIdType.MESH
F32, BF16 = jnp.float32, jnp.bfloat16
COMP = 3
LENGTH = 600
SEG = 4096
HALO = 768
WIDE = SEG + HALO
TAPS = 768
SPREAD = 256
SHARE = 32
HALF = 16
SUB = 8
ROWS = 256
ORDER = (6, 7, 5, 2, 4, 3, 1)
NEAR = (6, 7, 5, 2, 4, 3, 1, 0)


def gather_kernel(rec_hbm, tmpl_hbm, mov_hbm, all_ref, filt_ref, pick_ref, tmpl_ref, mov_row, mov_ref, pad, send, recv, home):
    s, t = lax.axis_index("sta"), lax.axis_index("tpl")
    h = lax.rem(s, 2)
    barrier = pltpu.get_barrier_semaphore()
    for i in ORDER:
        pl.semaphore_signal(barrier, inc=1, device_id=(s, t ^ i), device_id_type=MESH)

    own = pltpu.make_async_copy(rec_hbm, all_ref.at[t], home.at[0])
    own.start()
    tmpl = pltpu.make_async_copy(tmpl_hbm, tmpl_ref, home.at[1])
    tmpl.start()
    shift = pltpu.make_async_copy(mov_hbm, mov_row, home.at[2])
    shift.start()
    pad[...] = jnp.zeros_like(pad)
    shift.wait()
    square = (SHARE, SHARE)
    diagonal = lax.broadcasted_iota(jnp.int32, square, 0) == lax.broadcasted_iota(jnp.int32, square, 1)
    mov_ref[...] = jnp.sum(jnp.where(diagonal, jnp.broadcast_to(mov_row[...], square), 0), axis=1, keepdims=True)
    moves = jnp.broadcast_to(mov_ref[...], (SHARE, TAPS))

    def filters(c):
        shape = tmpl_ref[c].astype(F32)
        factor = lax.rsqrt(jnp.sum(shape * shape, axis=1, keepdims=True) / LENGTH + 1e-05)
        pad[:, :LENGTH] = (shape * factor).astype(BF16).astype(F32)
        unit = pad[...]
        for bit in range(6):
            moved = pltpu.roll(unit, 2 << bit, 1)
            unit = jnp.where((moves & (1 << bit)) != 0, moved, unit)
        pad[...] = unit
        for part in range(2):
            first = pl.multiple_of(lax.rem(h + part, 2) * HALF, HALF)
            rows = pad[pl.ds(first, HALF), :]
            for b in range(SUB):
                moved = pltpu.roll(rows, 2 * b, 1) if b else rows
                at = part * HALF * SUB + b * HALF
                filt_ref[c, at : at + HALF, :] = moved.astype(BF16)
        pad[...] = jnp.zeros_like(pad)

    own.wait()
    pl.semaphore_wait(barrier, 7)
    copies = []
    for i in ORDER:
        copy = pltpu.make_async_remote_copy(
            src_ref=all_ref.at[t],
            dst_ref=all_ref.at[t],
            send_sem=send.at[i],
            recv_sem=recv.at[t],
            device_id=(s, t ^ i),
            device_id_type=MESH,
        )
        copy.start()
        copies.append(copy)
    tmpl.wait()
    for c in range(COMP):
        filters(c)
    lanes = lax.broadcasted_iota(jnp.int32, (HALF, SPREAD), 1) >> 1
    for part in range(2):
        first = pl.multiple_of(lax.rem(h + part, 2) * HALF, HALF)
        offsets = jnp.broadcast_to(mov_ref[pl.ds(first, HALF), :], (HALF, SPREAD))
        for b in range(SUB):
            at = part * HALF * SUB + b * HALF
            pick_ref[at : at + HALF, :] = jnp.where(lanes == offsets + b, 1.0, 0.0).astype(BF16)
    for copy in copies:
        copy.wait_send()
    for i in ORDER:
        source = t ^ i
        pltpu.make_async_remote_copy(
            src_ref=all_ref.at[t],
            dst_ref=all_ref.at[source],
            send_sem=send.at[i],
            recv_sem=recv.at[source],
            device_id=(s, source),
            device_id_type=MESH,
        ).wait_recv()


def gathered(rec, tmpl, mov):
    return pl.pallas_call(
        gather_kernel,
        out_shape=(
            jax.ShapeDtypeStruct((8, COMP, SEG), BF16),
            jax.ShapeDtypeStruct((COMP, ROWS, TAPS), BF16),
            jax.ShapeDtypeStruct((ROWS, SPREAD), BF16),
        ),
        in_specs=[pl.BlockSpec(memory_space=pltpu.HBM)] * 3,
        out_specs=[pl.BlockSpec(memory_space=pltpu.VMEM)] * 3,
        scratch_shapes=[
            pltpu.VMEM((COMP, SHARE, LENGTH), BF16),
            pltpu.VMEM((1, SHARE), jnp.int32),
            pltpu.VMEM((SHARE, 1), jnp.int32),
            pltpu.VMEM((SHARE, TAPS), F32),
            pltpu.SemaphoreType.DMA((8,)),
            pltpu.SemaphoreType.DMA((8,)),
            pltpu.SemaphoreType.DMA((3,)),
        ],
        compiler_params=pltpu.CompilerParams(collective_id=1, has_side_effects=True, vmem_limit_bytes=32 << 20),
    )(rec, tmpl, mov)


def shifted_rows(row):
    wide = jnp.broadcast_to(row, (8, WIDE))
    low = pltpu.roll(wide, WIDE - 112, 1, stride=16, stride_axis=0)
    return jnp.concatenate([low[:, : WIDE - 128], low[:, 128:]], axis=0).astype(BF16)


def energy_scales(x):
    def ahead(v, n):
        return pltpu.roll(v, WIDE - n, 1)

    power = x * x
    two = power + ahead(power, 1)
    four = two + ahead(two, 2)
    eight = four + ahead(four, 4)
    sixteen = eight + ahead(eight, 8)
    far = sixteen + ahead(eight, 16)
    w32 = sixteen + ahead(sixteen, 16)
    w64 = w32 + ahead(w32, 32)
    w128 = w64 + ahead(w64, 64)
    w256 = w128 + ahead(w128, 128)
    w512 = w256 + ahead(w256, 256)
    energy = w512 + ahead(w64, 512) + ahead(far, 576)
    scale = lax.rsqrt(energy / LENGTH + 1e-05) / LENGTH
    high = scale.astype(BF16).astype(F32)
    low = (scale - high).astype(BF16).astype(F32)
    odd = (lax.broadcasted_iota(jnp.int32, x.shape, 1) & 1) == 1
    return jnp.where(odd, pltpu.roll(low, 1, 1), high)


def scan_kernel(all_ref, filt_ref, pick_ref, out_ref, x8, z8, base, own, part_out, part_in, sum_out, sum_in, cs, cr, ss, sr):
    s, t = lax.axis_index("sta"), lax.axis_index("tpl")
    h = lax.rem(s, 2)
    pair = lax.div(s, 2)
    sibling = (s + 1 - 2 * h, t)
    barrier = pltpu.get_barrier_semaphore()
    pl.semaphore_signal(barrier, inc=1, device_id=sibling, device_id_type=MESH)
    for i in NEAR:
        j = pair ^ i

        @pl.when(jnp.logical_not((j == pair) & (pair == t)))
        def _():
            pl.semaphore_signal(barrier, inc=1, device_id=(2 * j + h, pair), device_id_type=MESH)

    for seg in range(8):
        block = all_ref[seg].astype(F32)
        for c in range(COMP):
            x8[c, seg : seg + 1, :SEG] = block[c : c + 1, :]
            if seg:
                x8[c, seg - 1 : seg, SEG:] = block[c : c + 1, :HALO]
    for c in range(COMP):
        x8[c, 7:8, SEG:] = jnp.zeros((1, HALO), F32)
    for c in range(COMP):
        z8[c] = energy_scales(x8[c])

    def core_copy(q):
        return pltpu.make_async_remote_copy(
            src_ref=part_out.at[q],
            dst_ref=part_in.at[q],
            send_sem=cs.at[q],
            recv_sem=cr.at[q],
            device_id=sibling,
            device_id_type=MESH,
        )

    def sum_copy(q):
        return pltpu.make_async_remote_copy(
            src_ref=sum_out.at[q],
            dst_ref=sum_in.at[pair],
            send_sem=ss.at[q],
            recv_sem=sr.at[pair],
            device_id=(2 * t + h, lax.rem(pair + q, 8)),
            device_id_type=MESH,
        )

    def compute(q):
        seg = lax.rem(pair + q, 8)
        for c in range(COMP):
            base[c, :, : WIDE - 128] = shifted_rows(x8[c, pl.ds(seg, 1), :])
            base[COMP + c, :, : WIDE - 128] = shifted_rows(z8[c, pl.ds(seg, 1), :])
        total = None
        for c in range(COMP):
            windows = jnp.concatenate([base[c, :, 256 * a : 256 * a + TAPS] for a in range(16)], axis=0)
            near = jnp.concatenate([base[COMP + c, :, 256 * a : 256 * a + SPREAD] for a in range(16)], axis=0)
            dims = (((1,), (1,)), ((), ()))
            number = lax.dot_general(windows, filt_ref[c], dims, preferred_element_type=F32)
            scale = lax.dot_general(near, pick_ref[...], dims, preferred_element_type=F32)
            term = number * scale
            total = term if total is None else total + term
        own[q] = total[:, :128]
        part_out[q] = total[:, 128:].astype(BF16)

    def finish(q):
        core_copy(q).wait_recv()
        both = (own[q] + part_in[q].astype(F32)).astype(BF16)
        seg = lax.rem(pair + q, 8)
        mine = (pair == t) & (seg == t)

        @pl.when(mine)
        def _():
            sum_in[pair] = both

        @pl.when(jnp.logical_not(mine))
        def _():
            sum_out[q] = both
            sum_copy(q).start()

    compute(0)
    pl.semaphore_wait(barrier, 9 - (pair == t).astype(jnp.int32))
    core_copy(0).start()

    compute(1)
    core_copy(1).start()

    @pl.loop(2, 8)
    def _(q):
        compute(q)
        core_copy(q).start()
        finish(q - 2)

    finish(6)
    finish(7)

    @pl.loop(0, 8)
    def _(q):
        core_copy(q).wait_send()

        @pl.when(jnp.logical_not((pair == t) & (lax.rem(pair + q, 8) == t)))
        def _():
            sum_copy(q).wait_send()

    for j in range(8):

        @pl.when(jnp.logical_not((j == pair) & (pair == t)))
        def _():
            pltpu.make_async_remote_copy(
                src_ref=sum_out.at[j],
                dst_ref=sum_in.at[j],
                send_sem=ss.at[j],
                recv_sem=sr.at[j],
                device_id=(2 * t + h, t),
                device_id_type=MESH,
            ).wait_recv()

    total = sum_in[0].astype(F32)
    for j in range(1, 8):
        total = total + sum_in[j].astype(F32)
    out_ref[...] = total


def scanned(everything, filters, picks):
    return pl.pallas_call(
        scan_kernel,
        out_shape=jax.ShapeDtypeStruct((ROWS, 128), F32),
        in_specs=[pl.BlockSpec(memory_space=pltpu.VMEM)] * 3,
        out_specs=pl.BlockSpec(memory_space=pltpu.VMEM),
        scratch_shapes=[
            pltpu.VMEM((COMP, 8, WIDE), F32),
            pltpu.VMEM((COMP, 8, WIDE), F32),
            pltpu.VMEM((2 * COMP, 16, WIDE), BF16),
            pltpu.VMEM((8, ROWS, 128), F32),
            pltpu.VMEM((8, ROWS, 128), BF16),
            pltpu.VMEM((8, ROWS, 128), BF16),
            pltpu.VMEM((8, ROWS, 128), BF16),
            pltpu.VMEM((8, ROWS, 128), BF16),
            pltpu.SemaphoreType.DMA((8,)),
            pltpu.SemaphoreType.DMA((8,)),
            pltpu.SemaphoreType.DMA((8,)),
            pltpu.SemaphoreType.DMA((8,)),
        ],
        compiler_params=pltpu.CompilerParams(collective_id=2, has_side_effects=True, vmem_limit_bytes=48 << 20),
    )(everything, filters, picks)


def local(records, templates, moveouts):
    operands = (records[0], jnp.transpose(templates[:, 0], (1, 0, 2)), jnp.transpose(moveouts))
    everything, filters, picks = gathered(*[pltpu.with_memory_space_constraint(v, pltpu.HBM) for v in operands])
    sums = scanned(everything, filters, picks)
    parts = jnp.flip(sums.reshape(ROWS // 8, 8, SUB, HALF), axis=1)
    return jnp.transpose(parts, (3, 0, 1, 2)).reshape(HALF, ROWS * SUB)


def solution(mesh):
    return jax.shard_map(
        local,
        mesh=mesh,
        in_specs=(P("sta", None, "tpl"), P("tpl", "sta", None, None), P("tpl", "sta")),
        out_specs=P("sta", "tpl"),
        check_vma=False,
    )
```

```python
import functools

import jax
import jax.numpy as jnp
from jax import lax
from jax.experimental import pallas as pl
from jax.experimental.pallas import tpu as pltpu
from jax.sharding import PartitionSpec as P

MESH = pl.DeviceIdType.MESH
F32, BF16 = jnp.float32, jnp.bfloat16
COMP = 3
LENGTH = 600
SEG = 4096
HALO = 768
WIDE = SEG + HALO
TAPS = 768
SPREAD = 256
SHARE = 32
HALF = 16
SUB = 8
ROWS = 256
ORDER = (6, 7, 5, 2, 4, 3, 1)
NEAR = (6, 7, 5, 2, 4, 3, 1, 0)


def gather_kernel(rec_hbm, tmpl_hbm, mov_hbm, all_ref, filt_ref, pick_ref, tmpl_ref, mov_row, mov_ref, pad, send, recv, home):
    s, t = lax.axis_index("sta"), lax.axis_index("tpl")
    h = lax.rem(s, 2)
    barrier = pltpu.get_barrier_semaphore()
    for i in ORDER:
        pl.semaphore_signal(barrier, inc=1, device_id=(s, t ^ i), device_id_type=MESH)

    own = pltpu.make_async_copy(rec_hbm, all_ref.at[t], home.at[0])
    own.start()
    tmpl = pltpu.make_async_copy(tmpl_hbm, tmpl_ref, home.at[1])
    tmpl.start()
    shift = pltpu.make_async_copy(mov_hbm, mov_row, home.at[2])
    shift.start()
    pad[...] = jnp.zeros_like(pad)
    shift.wait()
    square = (SHARE, SHARE)
    diagonal = lax.broadcasted_iota(jnp.int32, square, 0) == lax.broadcasted_iota(jnp.int32, square, 1)
    mov_ref[...] = jnp.sum(jnp.where(diagonal, jnp.broadcast_to(mov_row[...], square), 0), axis=1, keepdims=True)
    moves = jnp.broadcast_to(mov_ref[...], (SHARE, TAPS))

    def filters(c):
        shape = tmpl_ref[c].astype(F32)
        factor = lax.rsqrt(jnp.sum(shape * shape, axis=1, keepdims=True) / LENGTH + 1e-05)
        pad[:, :LENGTH] = (shape * factor).astype(BF16).astype(F32)
        unit = pad[...]
        for bit in range(6):
            moved = pltpu.roll(unit, 2 << bit, 1)
            unit = jnp.where((moves & (1 << bit)) != 0, moved, unit)
        pad[...] = unit
        for part in range(2):
            first = pl.multiple_of(lax.rem(h + part, 2) * HALF, HALF)
            rows = pad[pl.ds(first, HALF), :]
            for b in range(SUB):
                moved = pltpu.roll(rows, 2 * b, 1) if b else rows
                at = part * HALF * SUB + b * HALF
                filt_ref[c, at : at + HALF, :] = moved.astype(BF16)
        pad[...] = jnp.zeros_like(pad)

    own.wait()
    pl.semaphore_wait(barrier, 7)
    copies = []
    for i in ORDER:
        copy = pltpu.make_async_remote_copy(
            src_ref=all_ref.at[t],
            dst_ref=all_ref.at[t],
            send_sem=send.at[i],
            recv_sem=recv.at[t],
            device_id=(s, t ^ i),
            device_id_type=MESH,
        )
        copy.start()
        copies.append(copy)
    tmpl.wait()
    for c in range(COMP):
        filters(c)
    lanes = lax.broadcasted_iota(jnp.int32, (HALF, SPREAD), 1) >> 1
    for part in range(2):
        first = pl.multiple_of(lax.rem(h + part, 2) * HALF, HALF)
        offsets = jnp.broadcast_to(mov_ref[pl.ds(first, HALF), :], (HALF, SPREAD))
        for b in range(SUB):
            at = part * HALF * SUB + b * HALF
            pick_ref[at : at + HALF, :] = jnp.where(lanes == offsets + b, 1.0, 0.0).astype(BF16)
    for copy in copies:
        copy.wait_send()
    for i in ORDER:
        source = t ^ i
        pltpu.make_async_remote_copy(
            src_ref=all_ref.at[t],
            dst_ref=all_ref.at[source],
            send_sem=send.at[i],
            recv_sem=recv.at[source],
            device_id=(s, source),
            device_id_type=MESH,
        ).wait_recv()


def gathered(rec, tmpl, mov):
    return pl.pallas_call(
        gather_kernel,
        out_shape=(
            jax.ShapeDtypeStruct((8, COMP, SEG), BF16),
            jax.ShapeDtypeStruct((COMP, ROWS, TAPS), BF16),
            jax.ShapeDtypeStruct((ROWS, SPREAD), BF16),
        ),
        in_specs=[pl.BlockSpec(memory_space=pltpu.HBM)] * 3,
        out_specs=[pl.BlockSpec(memory_space=pltpu.VMEM)] * 3,
        scratch_shapes=[
            pltpu.VMEM((COMP, SHARE, LENGTH), BF16),
            pltpu.VMEM((1, SHARE), jnp.int32),
            pltpu.VMEM((SHARE, 1), jnp.int32),
            pltpu.VMEM((SHARE, TAPS), F32),
            pltpu.SemaphoreType.DMA((8,)),
            pltpu.SemaphoreType.DMA((8,)),
            pltpu.SemaphoreType.DMA((3,)),
        ],
        compiler_params=pltpu.CompilerParams(collective_id=1, has_side_effects=True, vmem_limit_bytes=32 << 20),
    )(rec, tmpl, mov)


def shifted_rows(row):
    wide = jnp.broadcast_to(row, (8, WIDE))
    low = pltpu.roll(wide, WIDE - 112, 1, stride=16, stride_axis=0)
    return jnp.concatenate([low[:, : WIDE - 128], low[:, 128:]], axis=0).astype(BF16)


def energy_scales(x):
    def ahead(v, n):
        return pltpu.roll(v, WIDE - n, 1)

    power = x * x
    two = power + ahead(power, 1)
    four = two + ahead(two, 2)
    eight = four + ahead(four, 4)
    sixteen = eight + ahead(eight, 8)
    far = sixteen + ahead(eight, 16)
    w32 = sixteen + ahead(sixteen, 16)
    w64 = w32 + ahead(w32, 32)
    w128 = w64 + ahead(w64, 64)
    w256 = w128 + ahead(w128, 128)
    w512 = w256 + ahead(w256, 256)
    energy = w512 + ahead(w64, 512) + ahead(far, 576)
    scale = lax.rsqrt(energy / LENGTH + 1e-05) / LENGTH
    high = scale.astype(BF16).astype(F32)
    low = (scale - high).astype(BF16).astype(F32)
    odd = (lax.broadcasted_iota(jnp.int32, x.shape, 1) & 1) == 1
    return jnp.where(odd, pltpu.roll(low, 1, 1), high)


def scan_kernel(all_ref, filt_ref, pick_ref, out_ref, x8, z8, base, own, part_out, part_in, sum_out, sum_in, cs, cr, ss, sr):
    s, t = lax.axis_index("sta"), lax.axis_index("tpl")
    h = lax.rem(s, 2)
    pair = lax.div(s, 2)
    sibling = (s + 1 - 2 * h, t)
    y_hi = lax.div(pair, 4)

    def chunk(q):
        return 4 * lax.rem(1 - y_hi + lax.div(q, 4), 2) + lax.rem(pair + q, 4)

    barrier = pltpu.get_barrier_semaphore()
    pl.semaphore_signal(barrier, inc=1, device_id=sibling, device_id_type=MESH)
    for i in NEAR:
        j = pair ^ i

        @pl.when(jnp.logical_not((j == pair) & (pair == t)))
        def _():
            pl.semaphore_signal(barrier, inc=1, device_id=(2 * j + h, pair), device_id_type=MESH)

    for seg in range(8):
        block = all_ref[seg].astype(F32)
        for c in range(COMP):
            x8[c, seg : seg + 1, :SEG] = block[c : c + 1, :]
            if seg:
                x8[c, seg - 1 : seg, SEG:] = block[c : c + 1, :HALO]
    for c in range(COMP):
        x8[c, 7:8, SEG:] = jnp.zeros((1, HALO), F32)
    for c in range(COMP):
        z8[c] = energy_scales(x8[c])

    def core_copy(q):
        return pltpu.make_async_remote_copy(
            src_ref=part_out.at[q],
            dst_ref=part_in.at[q],
            send_sem=cs.at[q],
            recv_sem=cr.at[q],
            device_id=sibling,
            device_id_type=MESH,
        )

    def sum_copy(q):
        return pltpu.make_async_remote_copy(
            src_ref=sum_out.at[q],
            dst_ref=sum_in.at[pair],
            send_sem=ss.at[q],
            recv_sem=sr.at[pair],
            device_id=(2 * t + h, chunk(q)),
            device_id_type=MESH,
        )

    def compute(q):
        seg = chunk(q)
        for c in range(COMP):
            base[c, :, : WIDE - 128] = shifted_rows(x8[c, pl.ds(seg, 1), :])
            base[COMP + c, :, : WIDE - 128] = shifted_rows(z8[c, pl.ds(seg, 1), :])
        total = None
        for c in range(COMP):
            windows = jnp.concatenate([base[c, :, 256 * a : 256 * a + TAPS] for a in range(16)], axis=0)
            near = jnp.concatenate([base[COMP + c, :, 256 * a : 256 * a + SPREAD] for a in range(16)], axis=0)
            dims = (((1,), (1,)), ((), ()))
            number = lax.dot_general(windows, filt_ref[c], dims, preferred_element_type=F32)
            scale = lax.dot_general(near, pick_ref[...], dims, preferred_element_type=F32)
            term = number * scale
            total = term if total is None else total + term
        own[q] = total[:, :128]
        part_out[q] = total[:, 128:].astype(BF16)

    def finish(q):
        core_copy(q).wait_recv()
        both = (own[q] + part_in[q].astype(F32)).astype(BF16)
        seg = chunk(q)
        mine = (pair == t) & (seg == t)

        @pl.when(mine)
        def _():
            sum_in[pair] = both

        @pl.when(jnp.logical_not(mine))
        def _():
            sum_out[q] = both
            sum_copy(q).start()

    compute(0)
    pl.semaphore_wait(barrier, 9 - (pair == t).astype(jnp.int32))
    core_copy(0).start()

    compute(1)
    core_copy(1).start()

    @pl.loop(2, 8)
    def _(q):
        compute(q)
        core_copy(q).start()
        finish(q - 2)

    finish(6)
    finish(7)

    @pl.loop(0, 8)
    def _(q):
        core_copy(q).wait_send()

        @pl.when(jnp.logical_not((pair == t) & (chunk(q) == t)))
        def _():
            sum_copy(q).wait_send()

    for j in range(8):

        @pl.when(jnp.logical_not((j == pair) & (pair == t)))
        def _():
            pltpu.make_async_remote_copy(
                src_ref=sum_out.at[j],
                dst_ref=sum_in.at[j],
                send_sem=ss.at[j],
                recv_sem=sr.at[j],
                device_id=(2 * t + h, t),
                device_id_type=MESH,
            ).wait_recv()

    total = sum_in[0].astype(F32)
    for j in range(1, 8):
        total = total + sum_in[j].astype(F32)
    out_ref[...] = total


def scanned(everything, filters, picks):
    return pl.pallas_call(
        scan_kernel,
        out_shape=jax.ShapeDtypeStruct((ROWS, 128), F32),
        in_specs=[pl.BlockSpec(memory_space=pltpu.VMEM)] * 3,
        out_specs=pl.BlockSpec(memory_space=pltpu.VMEM),
        scratch_shapes=[
            pltpu.VMEM((COMP, 8, WIDE), F32),
            pltpu.VMEM((COMP, 8, WIDE), F32),
            pltpu.VMEM((2 * COMP, 16, WIDE), BF16),
            pltpu.VMEM((8, ROWS, 128), F32),
            pltpu.VMEM((8, ROWS, 128), BF16),
            pltpu.VMEM((8, ROWS, 128), BF16),
            pltpu.VMEM((8, ROWS, 128), BF16),
            pltpu.VMEM((8, ROWS, 128), BF16),
            pltpu.SemaphoreType.DMA((8,)),
            pltpu.SemaphoreType.DMA((8,)),
            pltpu.SemaphoreType.DMA((8,)),
            pltpu.SemaphoreType.DMA((8,)),
        ],
        compiler_params=pltpu.CompilerParams(collective_id=2, has_side_effects=True, vmem_limit_bytes=48 << 20),
    )(everything, filters, picks)


def local(records, templates, moveouts):
    operands = (records[0], jnp.transpose(templates[:, 0], (1, 0, 2)), jnp.transpose(moveouts))
    everything, filters, picks = gathered(*[pltpu.with_memory_space_constraint(v, pltpu.HBM) for v in operands])
    sums = scanned(everything, filters, picks)
    parts = jnp.flip(sums.reshape(ROWS // 8, 8, SUB, HALF), axis=1)
    return jnp.transpose(parts, (3, 0, 1, 2)).reshape(HALF, ROWS * SUB)


def solution(mesh):
    return jax.shard_map(
        local,
        mesh=mesh,
        in_specs=(P("sta", None, "tpl"), P("tpl", "sta", None, None), P("tpl", "sta")),
        out_specs=P("sta", "tpl"),
        check_vma=False,
    )
```
